32 devices in a mesh: groups: 2 (over y), frames: 4 (over z), rows: 2 (over x), heads: 2 (over core).
Axes of the slice: x: 2, y: 2, z: 4, core: 2. Of those that a mesh axis runs over, the one named last changes fastest.
Arguments:
- queries: bfloat16 [8, 16, 64, 2240], P(('groups', 'frames'), 'rows', None, 'heads'), parts along dimension 0, may hold values from -2 to 1
- keys: bfloat16 [8, 16, 64, 2240], P(('groups', 'frames'), 'rows', None, 'heads'), parts along dimension 0, may hold values from -6 to 6
- values: bfloat16 [8, 16, 64, 2240], P(('groups', 'frames'), 'rows', None, 'heads'), parts along dimension 0, may hold values from -20 to 20
- out_weight: bfloat16 [2240, 2240], P('heads', 'frames'), may hold values from -0.125 to 0.125
Outputs:
- projected: bfloat16 [8, 16, 64, 2240], P(('groups', 'frames'), 'rows', None, 'heads'), parts along dimension 0
The draws below stay inside these ranges and needn't reach their ends.
There are 2 independent parts, one for each index of `groups`. The reference program is written for one: setup_inputs(seed, part) draws one part's arguments, and reference() takes and returns one part's arrays. A program takes and returns all parts, laid end to end along the dimension named above; an argument that names none is the same for every part. Nothing has to cross between parts.
All inputs are finite; a program needn't handle non-finite values.
Results may differ from the reference program's by a relative error of at most 0.0049.
Values may be sent and summed in bfloat16 or wider, within the bound.
A program may use at most 64 MiB of HBM per device.

```python
import jax
import jax.numpy as jnp
from jax import lax

D = 2240
HD = 112
WIDTH = 64
ROW_DEV = 8
FRAMES = 4
HEIGHT = 16


def draw_pair(key):
    base = jax.random.fold_in(key, 7)
    key_key, noise_key, shift_key = jax.random.split(base, 3)
    blocks = HEIGHT // ROW_DEV
    key_field = jnp.clip(jax.random.normal(key_key, (FRAMES, HEIGHT, WIDTH, D), jnp.float32), -6.0, 6.0)
    noise = jax.random.normal(noise_key, (FRAMES, HEIGHT, WIDTH, D), jnp.float32)
    shifts = 2.0 * jax.random.normal(shift_key, (FRAMES, blocks, 1, D), jnp.float32)
    shifts = jnp.repeat(shifts, ROW_DEV, axis=1)
    value_field = jnp.clip(3.0 * key_field + noise + shifts, -20.0, 20.0)
    return (key_field, value_field)


def draw_keys(key, part):
    return draw_pair(key)[0].astype(jnp.bfloat16)


def draw_values(key, part):
    return draw_pair(key)[1].astype(jnp.bfloat16)


def shard_levels(rng, extent, cuts, smallest, top_value):
    loudness = 1.0
    for position, parts in cuts:
        draws = jax.random.uniform(jax.random.fold_in(jax.random.fold_in(rng, 6), position), (parts,), jnp.float32, smallest / len(cuts), top_value / len(cuts))
        loudness = loudness * jnp.repeat(jnp.exp(draws), extent[position] // parts).reshape((-1,) + (1,) * (len(extent) - 1 - position))
    return loudness


def gaussian(key, shape, width, most, pieces=(), held_as=jnp.bfloat16):
    level = shard_levels(key, shape, pieces, -0.22, 0.18) if pieces else 1.0
    array = jax.random.normal(key, shape, jnp.float32) * width * level
    return jnp.minimum(jnp.maximum(array, -most), most).astype(held_as)


def setup_inputs(seed: int = 0, part: int = 0) -> dict:
    key_of = jax.random.split(jax.random.key(seed), 5)
    own_keys = jax.random.split(jax.random.fold_in(key_of[4], part), 5)
    return {
        "queries": jnp.clip(-2.0 + 3.0 * jax.random.uniform(own_keys[0], (FRAMES, HEIGHT, WIDTH, D), jnp.float32) ** shard_levels(own_keys[0], (FRAMES, HEIGHT, WIDTH, D), ((0, 4), (1, 2), (3, 2)), -0.2, 0.2), -2.0, 1.0).astype(jnp.bfloat16),
        "keys": draw_keys(jax.random.fold_in(jax.random.fold_in(key_of[4], part), 71), part),
        "values": draw_values(jax.random.fold_in(jax.random.fold_in(key_of[4], part), 71), part),
        "out_weight": gaussian(key_of[3], (D, D), D ** -0.5, 0.125, ((0, 2), (1, 4))),
    }


EPS = 1e-6


def reference(queries, keys, values, out_weight):
    frames_all, height_all, width_all, features = queries.shape
    heads = features // HD
    shape4 = (frames_all, height_all * width_all, heads, HD)
    query_pos = jnp.maximum(queries, 0).reshape(shape4).astype(jnp.float32)
    key_pos = jnp.maximum(keys, 0).reshape(shape4).astype(jnp.float32)
    value_rows = values.reshape(shape4).astype(jnp.float32)
    frame_state = jnp.einsum("fthd,fthe->fhde", key_pos, value_rows, precision=lax.Precision.HIGHEST)
    frame_norm = jnp.sum(key_pos, axis=1)
    state = jnp.cumsum(frame_state, axis=0)
    norm = jnp.cumsum(frame_norm, axis=0)
    numer = jnp.einsum("fthd,fhde->fthe", query_pos, state, precision=lax.Precision.HIGHEST)
    denom = jnp.einsum("fthd,fhd->fth", query_pos, norm, precision=lax.Precision.HIGHEST)
    attended = (numer / (denom[..., None] + EPS)).astype(jnp.bfloat16)
    attended = attended.reshape(frames_all * height_all * width_all, features)
    projected = jnp.dot(attended, out_weight, preferred_element_type=jnp.float32).astype(jnp.bfloat16)
    return projected.reshape(frames_all, height_all, width_all, features)
```

```python
import functools

import jax
import jax.numpy as jnp
from jax import lax
from jax.experimental import pallas as pl
from jax.experimental.pallas import tpu as pltpu
from jax.sharding import PartitionSpec as P

HD = 112
EPS = 1e-06
LANES = 128
MESH = pl.DeviceIdType.MESH


def prefix_before(local):
    position = lax.axis_index("frames") * local[0].shape[0]
    pieces = (
        lax.all_gather(local[0], "frames", axis=0, tiled=True),
        lax.all_gather(local[1], "frames", axis=0, tiled=True),
    )
    count = pieces[0].shape[0]
    keep = jnp.arange(count, dtype=jnp.int32) < position
    states = jnp.sum(jnp.where(keep[:, None, None, None], pieces[0], 0.0), axis=0, keepdims=True)
    totals = jnp.sum(jnp.where(keep[:, None, None], pieces[1], 0.0), axis=0, keepdims=True)
    return (states, totals)


def general(queries, keys, values, out_weight):
    frames_here, rows_here, columns, features = queries.shape
    heads_here = features // HD
    shape4 = (frames_here, rows_here * columns, heads_here, HD)
    query_pos = jnp.maximum(queries, 0).reshape(shape4).astype(jnp.float32)
    key_pos = jnp.maximum(keys, 0).reshape(shape4)
    value_rows = values.reshape(shape4)
    frame_state = jnp.einsum(
        "fthd,fthe->fhde", key_pos, value_rows, preferred_element_type=jnp.float32
    )
    frame_norm = jnp.sum(key_pos.astype(jnp.float32), axis=1)
    own = lax.psum((frame_state, frame_norm), "rows")
    earlier = prefix_before(own)
    state = own[0] + earlier[0]
    norm = own[1] + earlier[1]
    numer = jnp.einsum("fthd,fhde->fthe", query_pos, state, precision=lax.Precision.HIGHEST)
    denom = jnp.einsum("fthd,fhd->fth", query_pos, norm, precision=lax.Precision.HIGHEST)
    attended = (numer / (denom[..., None] + EPS)).astype(jnp.bfloat16)
    attended = attended.reshape(frames_here * rows_here * columns, features)
    terms = jnp.dot(
        attended,
        lax.all_gather(out_weight, "frames", axis=1, tiled=True),
        preferred_element_type=jnp.float32,
    )
    mixed = lax.psum_scatter(terms, "heads", scatter_dimension=1, tiled=True).astype(jnp.bfloat16)
    return mixed.reshape(frames_here, rows_here, columns, mixed.shape[1])


A, D, X, Y = 0, 1, 2, 3
PIECES = 5
OVER_Z, OVER_X, LAG = 1, 2, 3


def kernel(
    nz, q_hbm, k_hbm, v_hbm, w_ref, out_ref,
    q_ref, k_ref, v_ref, kt, wbuf, att, st, acc, rs_send, rs_recv, hand, z_recv, fin_send, fin, fmat, nmat,
    in_sem, w_recv, own_send, rel_send, block_sem, rs_out, rs_in, hand_out, hand_in, z_out, z_in,
    ag_out, give_out, fin_in, at_out, at_in,
):
    y, z = lax.axis_index("groups"), lax.axis_index("frames")
    x, c = lax.axis_index("rows"), lax.axis_index("heads")
    chunks = w_ref.shape[0]
    tokens, features = q_ref.shape
    wide = w_ref.shape[0] * w_ref.shape[1]
    heads = features // HD
    half = heads // 2
    parts = chunks // 2
    slots = nz // 2
    home = z // slots
    relays = c == x
    f32, bf16 = jnp.float32, jnp.bfloat16

    def dev(x_=None, y_=None, z_=None, c_=None):
        return (
            y if y_ is None else y_,
            z if z_ is None else z_,
            x if x_ is None else x_,
            c if c_ is None else c_,
        )

    partner = dev(c_=1 - c)
    barrier = pltpu.get_barrier_semaphore()

    def greet(device):
        pl.semaphore_signal(barrier, inc=1, device_id=device, device_id_type=MESH)

    greet(partner)
    for core in range(2):
        greet(dev(x_=1 - x, c_=core))
        greet(dev(y_=1 - y, c_=core))
    for side in (-1, 1):
        @pl.when((z + side >= 0) & (z + side < nz))
        def _():
            for core in range(2):
                greet(dev(z_=z + side, c_=core))

    loads = [
        pltpu.make_async_copy(src, dst, in_sem.at[n])
        for n, (src, dst) in enumerate(((k_hbm, k_ref), (v_hbm, v_ref), (q_hbm, q_ref)))
    ]
    for load in loads:
        load.start()

    pl.semaphore_wait(barrier, jnp.where((z > 0) & (z < nz - 1), 9, 7))

    def remote(src, dst, send, recv, device):
        return pltpu.make_async_remote_copy(
            src_ref=src, dst_ref=dst, send_sem=send, recv_sem=recv,
            device_id=device, device_id_type=MESH,
        )

    def each(count, act, begin=0):
        def body(j, carry):
            act(j)
            return carry
        lax.fori_loop(begin, count, body, 0)

    def when(wanted, act):
        @pl.when(wanted)
        def _():
            act()

    mine = lax.rem(x + y + c, 2)
    kind = jnp.where(relays, A, D)

    def own_copy(side, j):
        chunk = mine * parts + j
        return remote(
            w_ref.at[chunk],
            wbuf.at[z, c, chunk],
            own_send.at[side, j],
            w_recv.at[z, kind, j],
            dev(z_=z + 1 - 2 * side, c_=x),
        )

    def own_each(act):
        for side in range(2):
            @pl.when((z < nz - 1) if side == 0 else (z > 0))
            def _():
                each(parts, lambda j: act(own_copy(side, j)))

    when(relays, lambda: own_each(lambda copy: copy.start()))

    def near_copy(j):
        chunk = mine * parts + j
        return remote(
            w_ref.at[chunk],
            wbuf.at[z, c, chunk],
            own_send.at[2, j],
            w_recv.at[z, D, j],
            dev(z_=jnp.where(z == 1, 0, nz - 1), c_=home),
        )

    def near_each(act):
        @pl.when(jnp.logical_not(relays) & ((z == 1) | (z == nz - 2)))
        def _():
            each(OVER_Z, lambda j: act(near_copy(j)))

    near_each(lambda copy: copy.start())

    block_local = pltpu.make_async_copy(w_ref, wbuf.at[z, c], block_sem.at[0])
    block_out = remote(w_ref, wbuf.at[z, c], block_sem.at[1], block_sem.at[2], partner)
    when(home == c, block_local.start)
    when(home != c, block_out.start)

    base = {A: (x, y * parts), D: (1 - x, (1 - y) * parts),
            X: (1 - x, y * parts), Y: (x, (1 - y) * parts)}

    def relay(s, what, j, lane, to_kind, device):
        rows, first = base[what]
        ref = wbuf.at[s, rows, first + j]
        return remote(ref, ref, rel_send.at[s, lane, j], w_recv.at[s, to_kind, j], device)

    def arrived(s, what, j):
        relay(s, what, j, 0, what, partner).wait_recv()

    def place(s):
        to = jnp.where(s < z, z + 1, z - 1)
        then = jnp.where(s < z, z + 2, z - 2)
        ends = (s == 0) | (s == nz - 1)
        more = (to >= 0) & (to < nz)
        last = (then < 0) | (then >= nz)
        return ends, more, last, jnp.clip(to, 0, nz - 1), s // slots

    edge = (z == 0) | (z == nz - 1)

    def split(s, j):
        direct = jnp.where(edge & (jnp.abs(s - z) == 1), OVER_Z, 0)
        plane = (s > 0) & (s < nz - 1) & (j >= direct)
        return plane & (j < direct + OVER_X), plane & (j >= direct + OVER_X)

    def sends_a(s, j):
        ends, more, last, to, at = place(s)
        over_x, over_y = split(s, j)
        x_core = jnp.where(over_y, 1 - x, at)
        y_core = jnp.where(over_x, x, at)
        return (
            (more, relay(s, A, j, 2, A, dev(z_=to, c_=x))),
            (None, relay(s, A, j, 0, X, dev(x_=1 - x, c_=x_core))),
            (None, relay(s, A, j, 1, Y, dev(y_=1 - y, c_=y_core))),
            (at != x, relay(s, A, j, 4, A, partner)),
        )

    def sends_d(s, j):
        ends, more, last, to, at = place(s)
        far = ends & more
        over_x, over_y = split(s, j)
        z_core = jnp.where(last, at, x)
        return (
            (over_x, Y, relay(s, Y, j, 3, D, dev(x_=1 - x, c_=at)), relay(s, Y, j, 5, Y, partner)),
            (over_y, X, relay(s, X, j, 3, D, dev(y_=1 - y, c_=at)), relay(s, X, j, 5, X, partner)),
            (far, D, relay(s, D, j, 3, D, dev(z_=to, c_=z_core)), relay(s, D, j, 5, D, partner)),
        ), at != x

    def around(d, act):
        for side in (-1, 1):
            s = z + side * d
            when((s >= 0) & (s < nz), lambda: act(jnp.clip(s, 0, nz - 1)))

    def on_a(s, j):
        arrived(s, A, j)
        for needed, copy in sends_a(s, j):
            if needed is None:
                copy.start()
            else:
                when(needed, copy.start)

    def on_d(s, j):
        options, share = sends_d(s, j)
        for wanted, what, copy, inner in options:
            @pl.when(wanted)
            def _():
                arrived(s, what, j)
                copy.start()
                when(share, inner.start)

    def drain(s, j):
        for needed, copy in sends_a(s, j):
            if needed is None:
                copy.wait_send()
            else:
                when(needed, copy.wait_send)
        options, share = sends_d(s, j)
        for wanted, what, copy, inner in options:
            @pl.when(wanted)
            def _():
                copy.wait_send()
                when(share, inner.wait_send)

    def rs(j):
        return remote(rs_send.at[(1 - x) * half + j], rs_recv.at[c, j], rs_out.at[j], rs_in.at[c, j],
                      dev(x_=1 - x, c_=x))

    def give(j):
        return remote(rs_send.at[x * half + j], hand.at[j], hand_out.at[j], hand_in.at[j], partner)

    loads[0].wait()
    kt[...] = jnp.maximum(k_ref[...], 0).T
    loads[1].wait()
    ones = jnp.ones((tokens, LANES), bf16)
    for j in range(half):
        for h in (j, half + j):
            first = h * HD
            begin = first // LANES * LANES
            end = min(-(-(first + HD) // LANES) * LANES, features)
            kp = kt[first:first + HD, :]
            both = jnp.dot(kp, v_ref[:, begin:end], preferred_element_type=f32)
            total = jnp.dot(kp, ones, preferred_element_type=f32)
            st[h, :, :HD] = both[:, first - begin:first - begin + HD]
            st[h, :, HD:] = total[:, HD:]
            rs_send[h] = st[h].astype(bf16)
        rs(j).start()
        when(relays, give(j).start)

    fmat[...] = jnp.zeros_like(fmat)
    nmat[...] = jnp.zeros_like(nmat)

    def up(core, j):
        return remote(fin_send.at[core, j], z_recv.at[core, j], z_out.at[core, j], z_in.at[core, j],
                      dev(z_=jnp.minimum(z + 1, nz - 1)))

    def across(core, j):
        return remote(fin_send.at[core, j], fin.at[x * half + j], ag_out.at[core, j], fin_in.at[x * half + j],
                      dev(x_=1 - x, c_=core))

    def inner(core, j):
        return remote(fin_send.at[core, j], fin.at[x * half + j], give_out.at[j], fin_in.at[x * half + j],
                      partner)

    def gather_step(j):
        for core in range(2):
            pltpu_wait = remote(rs_recv.at[core, j], rs_recv.at[core, j], rs_out.at[j], rs_in.at[core, j], partner)
            pltpu_wait.wait_recv()

            @pl.when(c == core)
            def _():
                acc[core, j] = st[x * half + j] + rs_recv[core, j].astype(f32)

            @pl.when(c != core)
            def _():
                give(j).wait_recv()
                acc[core, j] = hand[j].astype(f32) + rs_recv[core, j].astype(f32)

    def chain_step(j):
        for core in range(2):
            @pl.when(z > 0)
            def _():
                up(core, j).wait_recv()
                acc[core, j] = acc[core, j] + z_recv[core, j].astype(f32)
            fin_send[core, j] = acc[core, j].astype(bf16)
            when(z < nz - 1, up(core, j).start)
            across(core, j).start()

            @pl.when(c == core)
            def _():
                fin[x * half + j] = fin_send[core, j]
            when(c != core, inner(core, j).start)

    @pl.when(jnp.logical_not(relays))
    def _():
        each(half, gather_step)
        when(z == nz - 1, lambda: own_each(lambda copy: copy.start()))
        each(half, chain_step)
        when(z == 0, lambda: own_each(lambda copy: copy.start()))

    cuts = []
    for begin in range(0, features, 2 * LANES):
        end = min(begin + 2 * LANES, features)
        low = begin // HD * HD // LANES * LANES
        high = min(-(-(-(-end // HD) * HD) // LANES) * LANES, features)
        cuts.append((begin, end, low, high))

    def finished(i):
        ref = fin.at[i]
        remote(ref, ref, give_out.at[0], fin_in.at[i], partner).wait_recv()

    sections = ((0, 4 * LANES), (4 * LANES, features))

    def att_copy(n, rows):
        begin, end = sections[n]
        ref = att.at[rows, :, begin:end]
        return remote(ref, ref, at_out.at[n], at_in.at[n], partner)

    def attend():
        each(half, lambda j: finished((1 - x) * half + j))
        when(relays, lambda: each(half, lambda j: finished(x * half + j)))
        for h in range(heads):
            own = slice(h * HD, (h + 1) * HD)
            fmat[own, own] = fin[h, :, :HD]
            nmat[own, own] = jnp.broadcast_to(fin[h, :, HD:HD + 1], (HD, HD))
        sent = 0
        for begin, end, low, high in cuts:
            qp = jnp.maximum(q_ref[:, low:high], 0)
            numer = jnp.dot(qp, fmat[low:high, begin:end], preferred_element_type=f32)
            denom = jnp.dot(qp, nmat[low:high, begin:end], preferred_element_type=f32)
            att[c, :, begin:end] = (numer / (denom + EPS)).astype(bf16)
            if end == sections[sent][1]:
                att_copy(sent, c).start()
                sent += 1

    loads[2].wait()
    turn = jnp.where(relays, parts + (parts - 2) * z, 0)

    def step(t):
        d, j = t // parts + 1, lax.rem(t, parts)

        @pl.when(relays)
        def _():
            when(d < nz, lambda: around(d, lambda s: on_a(s, j)))
            late = t - LAG

            @pl.when(late >= 0)
            def _():
                around(late // parts + 1, lambda s: on_d(s, lax.rem(late, parts)))
        when(t == turn, attend)

    each((nz - 1) * parts + LAG, step)

    for n in range(len(sections)):
        att_copy(n, 1 - c).wait_recv()

    def slot(i):
        s = jnp.where(z <= slots * c, i, slots - 1 - i)
        return s, slots * c + s

    def landed(s, j, kinds):
        ends, more, last, to, at = place(s)
        over_x, over_y = split(s, j)
        held = {A: relays, X: relays & over_y, Y: relays & over_x, D: relays & ends & more}
        for what in kinds:
            when(jnp.logical_not(held[what]), lambda: arrived(s, what, j))

    def product(rows, weights):
        return lax.dot_general(att[rows], weights, (((1,), (1,)), ((), ())), preferred_element_type=f32)

    width = wide // 2
    for i in range(slots):
        s, source = slot(i)

        def quarter(rows, first):
            return wbuf[source, rows, pl.ds(first, parts)].reshape(width, features)

        def await_all(kinds):
            @pl.when(source != z)
            def _():
                each(parts, lambda j: landed(source, j, kinds))

        @pl.when(source == z)
        def _():
            block_local.wait()
            other = wbuf.at[z, 1 - c]
            remote(w_ref, other, block_sem.at[1], block_sem.at[2], partner).wait_recv()

        def put(side, value):
            value = value.astype(out_ref.dtype)
            for at in range(slots):
                for part in range(2):
                    first = (at * 2 + part) * width

                    @pl.when((s == at) & (side == part))
                    def _():
                        out_ref[:, first:first + width] = value

        await_all((A, X))
        put(y, product(x, quarter(x, y * parts)) + product(1 - x, quarter(1 - x, y * parts)))
        await_all((Y,))
        rest = product(x, quarter(x, (1 - y) * parts))
        await_all((D,))
        put(1 - y, rest + product(1 - x, quarter(1 - x, (1 - y) * parts)))

    near_each(lambda copy: copy.wait_send())
    when(relays | (z == 0) | (z == nz - 1), lambda: own_each(lambda copy: copy.wait_send()))
    when(home != c, block_out.wait_send)

    def sent(j):
        rs(j).wait_send()
        when(relays, give(j).wait_send)

        @pl.when(jnp.logical_not(relays))
        def _():
            for core in range(2):
                when(z < nz - 1, up(core, j).wait_send)
                across(core, j).wait_send()
                when(c != core, inner(core, j).wait_send)

    each(half, sent)
    for n in range(len(sections)):
        att_copy(n, c).wait_send()

    @pl.when(relays)
    def _():
        def drained(t):
            around(t // parts + 1, lambda s: drain(s, lax.rem(t, parts)))
        each((nz - 1) * parts, drained)


def fused(nz, queries, keys, values, out_weight):
    frames_here, rows_here, columns, features = queries.shape
    tokens = frames_here * rows_here * columns
    heads, half, wide = features // HD, features // HD // 2, out_weight.shape[1]
    slots = nz // 2
    chunks = 2 * PIECES
    parts = PIECES
    width = wide // chunks
    vmem, hbm = pl.BlockSpec(memory_space=pltpu.VMEM), pl.BlockSpec(memory_space=pl.ANY)
    bf16, f32 = jnp.bfloat16, jnp.float32
    dma = pltpu.SemaphoreType.DMA
    out = pl.pallas_call(
        functools.partial(kernel, nz),
        out_shape=jax.ShapeDtypeStruct((tokens, slots * wide), bf16),
        in_specs=[hbm] * 4,
        out_specs=vmem,
        scratch_shapes=[
            pltpu.VMEM((tokens, features), bf16),
            pltpu.VMEM((tokens, features), bf16),
            pltpu.VMEM((tokens, features), bf16),
            pltpu.VMEM((features, tokens), bf16),
            pltpu.VMEM((nz, 2, chunks, width, features), bf16),
            pltpu.VMEM((2, tokens, features), bf16),
            pltpu.VMEM((heads, HD, LANES), f32),
            pltpu.VMEM((2, half, HD, LANES), f32),
            pltpu.VMEM((heads, HD, LANES), bf16),
            pltpu.VMEM((2, half, HD, LANES), bf16),
            pltpu.VMEM((half, HD, LANES), bf16),
            pltpu.VMEM((2, half, HD, LANES), bf16),
            pltpu.VMEM((2, half, HD, LANES), bf16),
            pltpu.VMEM((heads, HD, LANES), bf16),
            pltpu.VMEM((features, features), bf16),
            pltpu.VMEM((features, features), bf16),
            dma((3,)),
            dma((nz, 4, parts)),
            dma((3, parts)),
            dma((nz, 6, parts)),
            dma((3,)),
            dma((half,)),
            dma((2, half)),
            dma((half,)),
            dma((half,)),
            dma((2, half)),
            dma((2, half)),
            dma((2, half)),
            dma((half,)),
            dma((heads,)),
            dma((2,)),
            dma((2,)),
        ],
        compiler_params=pltpu.CompilerParams(
            collective_id=0, has_side_effects=True, vmem_limit_bytes=56 * 2**20),
        name="attend_project",
    )(
        queries.reshape(tokens, features),
        keys.reshape(tokens, features),
        values.reshape(tokens, features),
        out_weight.T.reshape(chunks, width, features),
    )
    return out.reshape(frames_here, rows_here, columns, slots * wide)


def solution(mesh):
    size = dict(mesh.shape)
    pairs = size["rows"] == 2 and size["groups"] == 2 and size["heads"] == 2
    body = general
    if pairs and size["frames"] == 4:
        body = functools.partial(fused, size["frames"])
    return jax.shard_map(
        body,
        mesh=mesh,
        in_specs=(
            P(("groups", "frames"), "rows", None, "heads"),
            P(("groups", "frames"), "rows", None, "heads"),
            P(("groups", "frames"), "rows", None, "heads"),
            P("heads", "frames"),
        ),
        out_specs=P(("groups", "frames"), "rows", None, "heads"),
        check_vma=False,
    )
```

```python
import functools

import jax
import jax.numpy as jnp
from jax import lax
from jax.experimental import pallas as pl
from jax.experimental.pallas import tpu as pltpu
from jax.sharding import PartitionSpec as P

HD = 112
EPS = 1e-06
LANES = 128
MESH = pl.DeviceIdType.MESH


def prefix_before(local):
    position = lax.axis_index("frames") * local[0].shape[0]
    pieces = (
        lax.all_gather(local[0], "frames", axis=0, tiled=True),
        lax.all_gather(local[1], "frames", axis=0, tiled=True),
    )
    count = pieces[0].shape[0]
    keep = jnp.arange(count, dtype=jnp.int32) < position
    states = jnp.sum(jnp.where(keep[:, None, None, None], pieces[0], 0.0), axis=0, keepdims=True)
    totals = jnp.sum(jnp.where(keep[:, None, None], pieces[1], 0.0), axis=0, keepdims=True)
    return (states, totals)


def general(queries, keys, values, out_weight):
    frames_here, rows_here, columns, features = queries.shape
    heads_here = features // HD
    shape4 = (frames_here, rows_here * columns, heads_here, HD)
    query_pos = jnp.maximum(queries, 0).reshape(shape4).astype(jnp.float32)
    key_pos = jnp.maximum(keys, 0).reshape(shape4)
    value_rows = values.reshape(shape4)
    frame_state = jnp.einsum(
        "fthd,fthe->fhde", key_pos, value_rows, preferred_element_type=jnp.float32
    )
    frame_norm = jnp.sum(key_pos.astype(jnp.float32), axis=1)
    own = lax.psum((frame_state, frame_norm), "rows")
    earlier = prefix_before(own)
    state = own[0] + earlier[0]
    norm = own[1] + earlier[1]
    numer = jnp.einsum("fthd,fhde->fthe", query_pos, state, precision=lax.Precision.HIGHEST)
    denom = jnp.einsum("fthd,fhd->fth", query_pos, norm, precision=lax.Precision.HIGHEST)
    attended = (numer / (denom[..., None] + EPS)).astype(jnp.bfloat16)
    attended = attended.reshape(frames_here * rows_here * columns, features)
    terms = jnp.dot(
        attended,
        lax.all_gather(out_weight, "frames", axis=1, tiled=True),
        preferred_element_type=jnp.float32,
    )
    mixed = lax.psum_scatter(terms, "heads", scatter_dimension=1, tiled=True).astype(jnp.bfloat16)
    return mixed.reshape(frames_here, rows_here, columns, mixed.shape[1])


A, D, X, Y = 0, 1, 2, 3
PIECES = 5
OVER_Z, NEAR_X, FAR_X, LAG, LAG_Z = 1, 1, 2, 3, 4


def kernel(
    nz, q_hbm, k_hbm, v_hbm, w_ref, out_ref,
    q_ref, k_ref, v_ref, kt, wbuf, att, st, acc, rs_send, rs_recv, hand, z_recv, fin_send, fin, fmat, nmat,
    in_sem, w_recv, own_send, rel_send, block_sem, rs_out, rs_in, hand_out, hand_in, z_out, z_in,
    ag_out, fin_in, at_out, at_in,
):
    y, z = lax.axis_index("groups"), lax.axis_index("frames")
    x, c = lax.axis_index("rows"), lax.axis_index("heads")
    chunks = w_ref.shape[0]
    tokens, features = k_ref.shape
    wide = w_ref.shape[0] * w_ref.shape[1]
    heads = features // HD
    half = heads // 2
    parts = chunks // 2
    slots = nz // 2
    home = z // slots
    relays = c == x
    f32, bf16 = jnp.float32, jnp.bfloat16

    def dev(x_=None, y_=None, z_=None, c_=None):
        return (
            y if y_ is None else y_,
            z if z_ is None else z_,
            x if x_ is None else x_,
            c if c_ is None else c_,
        )

    def when(wanted, act):
        @pl.when(wanted)
        def _():
            act()

    partner = dev(c_=1 - c)
    barrier = pltpu.get_barrier_semaphore()

    def greet(device):
        pl.semaphore_signal(barrier, inc=1, device_id=device, device_id_type=MESH)

    greet(partner)
    for core in range(2):
        greet(dev(x_=1 - x, c_=core))
        greet(dev(y_=1 - y, c_=core))
    for side in (-1, 1):
        @pl.when((z + side >= 0) & (z + side < nz))
        def _():
            for core in range(2):
                greet(dev(z_=z + side, c_=core))

    loads = [
        pltpu.make_async_copy(src, dst, in_sem.at[n])
        for n, (src, dst) in enumerate(((k_hbm, k_ref), (v_hbm, v_ref), (q_hbm, q_ref.at[c])))
    ]
    loads[0].start()
    loads[1].start()
    when(c != x, loads[2].start)

    pl.semaphore_wait(barrier, jnp.where((z > 0) & (z < nz - 1), 9, 7))

    def remote(src, dst, send, recv, device):
        return pltpu.make_async_remote_copy(
            src_ref=src, dst_ref=dst, send_sem=send, recv_sem=recv,
            device_id=device, device_id_type=MESH,
        )

    def each(count, act, begin=0):
        def body(j, carry):
            act(j)
            return carry
        lax.fori_loop(begin, count, body, 0)

    mine = lax.rem(x + y + c, 2)
    kind = jnp.where(relays, A, D)

    def own_copy(side, j):
        chunk = mine * parts + j
        return remote(
            w_ref.at[chunk],
            wbuf.at[z, c, chunk],
            own_send.at[side, j],
            w_recv.at[z, kind, j],
            dev(z_=z + 1 - 2 * side, c_=x),
        )

    def own_each(act):
        for side in range(2):
            @pl.when((z < nz - 1) if side == 0 else (z > 0))
            def _():
                each(parts, lambda j: act(own_copy(side, j)))

    when(relays, lambda: own_each(lambda copy: copy.start()))

    def near_copy(j):
        chunk = mine * parts + j
        return remote(
            w_ref.at[chunk],
            wbuf.at[z, c, chunk],
            own_send.at[2, j],
            w_recv.at[z, D, j],
            dev(z_=jnp.where(z == 1, 0, nz - 1), c_=home),
        )

    def near_each(act):
        @pl.when(jnp.logical_not(relays) & ((z == 1) | (z == nz - 2)))
        def _():
            each(OVER_Z, lambda j: act(near_copy(j)))

    block_local = pltpu.make_async_copy(w_ref, wbuf.at[z, c], block_sem.at[0])
    block_out = remote(w_ref, wbuf.at[z, c], block_sem.at[1], block_sem.at[2], partner)
    lend = remote(q_hbm, q_ref.at[c], in_sem.at[3], in_sem.at[4], partner)
    when(relays, lend.start)
    when(home == c, block_local.start)
    when(home != c, block_out.start)

    base = {A: (x, y * parts), D: (1 - x, (1 - y) * parts),
            X: (1 - x, y * parts), Y: (x, (1 - y) * parts)}

    def relay(s, what, j, lane, to_kind, device):
        rows, first = base[what]
        ref = wbuf.at[s, rows, first + j]
        return remote(ref, ref, rel_send.at[s, lane, j], w_recv.at[s, to_kind, j], device)

    def arrived(s, what, j):
        relay(s, what, j, 0, what, partner).wait_recv()

    def place(s):
        to = jnp.where(s < z, z + 1, z - 1)
        then = jnp.where(s < z, z + 2, z - 2)
        ends = (s == 0) | (s == nz - 1)
        more = (to >= 0) & (to < nz)
        last = (then < 0) | (then >= nz)
        return ends, more, last, jnp.clip(to, 0, nz - 1), s // slots

    edge = (z == 0) | (z == nz - 1)

    def split(s, j):
        close = jnp.abs(s - z) == 1
        direct = jnp.where(edge & close, OVER_Z, 0)
        turned = direct + jnp.where(close, NEAR_X, FAR_X)
        plane = (s > 0) & (s < nz - 1) & (j >= direct)
        return plane & (j < turned), plane & (j >= turned)

    def sends_a(s, j):
        ends, more, last, to, at = place(s)
        over_x, over_y = split(s, j)
        x_core = jnp.where(over_y, 1 - x, at)
        y_core = jnp.where(over_x, x, at)
        return (
            (more, relay(s, A, j, 2, A, dev(z_=to, c_=x))),
            (None, relay(s, A, j, 0, X, dev(x_=1 - x, c_=x_core))),
            (None, relay(s, A, j, 1, Y, dev(y_=1 - y, c_=y_core))),
            (at != x, relay(s, A, j, 4, A, partner)),
        )

    def sends_d(s, j):
        ends, more, last, to, at = place(s)
        far = ends & more
        over_x, over_y = split(s, j)
        z_core = jnp.where(last, at, x)
        return (
            (over_x, Y, relay(s, Y, j, 3, D, dev(x_=1 - x, c_=at)), relay(s, Y, j, 5, Y, partner)),
            (over_y, X, relay(s, X, j, 3, D, dev(y_=1 - y, c_=at)), relay(s, X, j, 5, X, partner)),
            (far, D, relay(s, D, j, 3, D, dev(z_=to, c_=z_core)), relay(s, D, j, 5, D, partner)),
        ), at != x

    def around(d, act):
        for side in (-1, 1):
            s = z + side * d
            when((s >= 0) & (s < nz), lambda: act(jnp.clip(s, 0, nz - 1)))

    def on_a(s, j):
        arrived(s, A, j)
        for needed, copy in sends_a(s, j):
            if needed is None:
                copy.start()
            else:
                when(needed, copy.start)

    def on_d(s, j, along):
        options, share = sends_d(s, j)
        for wanted, what, copy, inner in options[2:] if along else options[:2]:
            @pl.when(wanted)
            def _():
                arrived(s, what, j)
                copy.start()
                when(share, inner.start)

    def drain(s, j):
        for needed, copy in sends_a(s, j):
            if needed is None:
                copy.wait_send()
            else:
                when(needed, copy.wait_send)
        options, share = sends_d(s, j)
        for wanted, what, copy, inner in options:
            @pl.when(wanted)
            def _():
                copy.wait_send()
                when(share, inner.wait_send)

    def rs(j):
        return remote(rs_send.at[(1 - x) * half + j], rs_recv.at[c, j], rs_out.at[j], rs_in.at[c, j],
                      dev(x_=1 - x, c_=x))

    def give(j):
        return remote(rs_send.at[x * half + j], hand.at[j], hand_out.at[j], hand_in.at[j], partner)

    loads[0].wait()
    kt[...] = jnp.maximum(k_ref[...], 0).T
    loads[1].wait()
    ones = jnp.ones((tokens, LANES), bf16)
    for j in range(half):
        for h in (j, half + j):
            first = h * HD
            begin = first // LANES * LANES
            end = min(-(-(first + HD) // LANES) * LANES, features)
            kp = kt[first:first + HD, :]
            both = jnp.dot(kp, v_ref[:, begin:end], preferred_element_type=f32)
            total = jnp.dot(kp, ones, preferred_element_type=f32)
            st[h, :, :HD] = both[:, first - begin:first - begin + HD]
            st[h, :, HD:] = total[:, HD:]
            rs_send[h] = st[h].astype(bf16)
        rs(j).start()
        when(relays, give(j).start)

    fmat[...] = jnp.zeros_like(fmat)
    nmat[...] = jnp.zeros_like(nmat)

    def up(core, j):
        return remote(fin_send.at[core, j], z_recv.at[core, j], z_out.at[core, j], z_in.at[core, j],
                      dev(z_=jnp.minimum(z + 1, nz - 1)))

    def across(core, j):
        return remote(fin_send.at[core, j], fin.at[core, x * half + j], ag_out.at[core, j], fin_in.at[core, j],
                      dev(x_=1 - x, c_=x))

    def gather_step(j):
        for core in range(2):
            pltpu_wait = remote(rs_recv.at[core, j], rs_recv.at[core, j], rs_out.at[j], rs_in.at[core, j], partner)
            pltpu_wait.wait_recv()

            @pl.when(c == core)
            def _():
                acc[core, j] = st[x * half + j] + rs_recv[core, j].astype(f32)

            @pl.when(c != core)
            def _():
                give(j).wait_recv()
                acc[core, j] = hand[j].astype(f32) + rs_recv[core, j].astype(f32)

    def chain_step(j):
        for core in range(2):
            @pl.when(z > 0)
            def _():
                up(core, j).wait_recv()
                acc[core, j] = acc[core, j] + z_recv[core, j].astype(f32)
            fin_send[core, j] = acc[core, j].astype(bf16)
            when(z < nz - 1, up(core, j).start)
            across(core, j).start()
            fin[core, x * half + j] = fin_send[core, j]

    @pl.when(jnp.logical_not(relays))
    def _():
        each(half, gather_step)
        when(z == nz - 1, lambda: own_each(lambda copy: copy.start()))
        each(half, chain_step)
        when(z == 0, lambda: own_each(lambda copy: copy.start()))

    cuts = []
    for begin in range(0, features, 2 * LANES):
        end = min(begin + 2 * LANES, features)
        low = begin // HD * HD // LANES * LANES
        high = min(-(-(-(-end // HD) * HD) // LANES) * LANES, features)
        cuts.append((begin, end, low, high))

    sections = ((0, 4 * LANES), (4 * LANES, features))

    def att_copy(n, rows):
        begin, end = sections[n]
        ref = att.at[rows, :, begin:end]
        return remote(ref, ref, at_out.at[rows, n], at_in.at[rows, n], partner)

    def attend(turn):
        rows = lax.rem(c + turn, 2)

        def finished(j):
            ref = fin.at[rows, (1 - x) * half + j]
            remote(ref, ref, ag_out.at[rows, j], fin_in.at[rows, j], partner).wait_recv()

        each(half, finished)
        for h in range(heads):
            own = slice(h * HD, (h + 1) * HD)
            block = fin[rows, h]
            fmat[own, own] = block[:, :HD]
            nmat[own, own] = jnp.broadcast_to(block[:, HD:HD + 1], (HD, HD))
        sent = 0
        for begin, end, low, high in cuts:
            qp = jnp.maximum(q_ref[rows, :, low:high], 0)
            numer = jnp.dot(qp, fmat[low:high, begin:end], preferred_element_type=f32)
            denom = jnp.dot(qp, nmat[low:high, begin:end], preferred_element_type=f32)
            att[rows, :, begin:end] = (numer / (denom + EPS)).astype(bf16)
            if end == sections[sent][1]:
                att_copy(sent, rows).start()
                sent += 1

    @pl.when(jnp.logical_not(relays))
    def _():
        loads[2].wait()
        remote(q_hbm, q_ref.at[1 - c], in_sem.at[3], in_sem.at[4], partner).wait_recv()
        each(2, attend)

    def step(t):
        d, j = t // parts + 1, lax.rem(t, parts)

        @pl.when(relays)
        def _():
            when(d < nz, lambda: around(d, lambda s: on_a(s, j)))
            for lag, along in ((LAG, False), (LAG_Z, True)):
                late = t - lag

                @pl.when((late >= 0) & (late < (nz - 1) * parts))
                def _():
                    around(late // parts + 1, lambda s: on_d(s, lax.rem(late, parts), along))

    each((nz - 1) * parts + max(LAG, LAG_Z), step)
    near_each(lambda copy: copy.start())

    @pl.when(relays)
    def _():
        for rows in range(2):
            for n in range(len(sections)):
                att_copy(n, rows).wait_recv()

    def slot(i):
        s = jnp.where(z <= slots * c, i, slots - 1 - i)
        return s, slots * c + s

    def landed(s, j, kinds):
        ends, more, last, to, at = place(s)
        over_x, over_y = split(s, j)
        held = {A: relays, X: relays & over_y, Y: relays & over_x, D: relays & ends & more}
        for what in kinds:
            when(jnp.logical_not(held[what]), lambda: arrived(s, what, j))

    def product(rows, weights):
        return lax.dot_general(att[rows], weights, (((1,), (1,)), ((), ())), preferred_element_type=f32)

    def drained(wanted, begin, end):
        @pl.when(relays & wanted)
        def _():
            each(end, lambda t: around(t // parts + 1, lambda s: drain(s, lax.rem(t, parts))), begin)

    width = wide // 2

    def quarter(source, rows, first):
        return wbuf[source, rows, pl.ds(first, parts)].reshape(width, features)

    def await_all(source, kinds):
        each(parts, lambda j: landed(source, j, kinds))

    def put(s, side, value):
        value = value.astype(out_ref.dtype)
        for at in range(slots):
            for part in range(2):
                first = (at * 2 + part) * width

                @pl.when((s == at) & (side == part))
                def _():
                    out_ref[:, first:first + width] = value

    def near(i):
        s, source = slot(i)
        await_all(source, (A, X))
        put(s, y, product(x, quarter(source, x, y * parts)) + product(1 - x, quarter(source, 1 - x, y * parts)))

    def distant(i):
        s, source = slot(i)
        await_all(source, (D,))
        rest = product(1 - x, quarter(source, 1 - x, (1 - y) * parts))
        await_all(source, (Y,))
        put(s, 1 - y, rest + product(x, quarter(source, x, (1 - y) * parts)))

    @pl.when(home == c)
    def _():
        s, source = slot(0)
        block_local.wait()
        other = wbuf.at[z, 1 - c]
        remote(w_ref, other, block_sem.at[1], block_sem.at[2], partner).wait_recv()
        out = product(0, wbuf[source, 0].reshape(wide, features))
        out = (out + product(1, wbuf[source, 1].reshape(wide, features))).astype(out_ref.dtype)
        for at in range(slots):
            @pl.when(s == at)
            def _():
                out_ref[:, at * wide:(at + 1) * wide] = out

    @pl.when(home != c)
    def _():
        near(0)

    drained(edge, 0, (nz - 2) * parts)
    when(home != c, lambda: distant(0))
    near(slots - 1)
    drained(edge, (nz - 2) * parts, (nz - 1) * parts)
    distant(slots - 1)

    near_each(lambda copy: copy.wait_send())
    when(relays | (z == 0) | (z == nz - 1), lambda: own_each(lambda copy: copy.wait_send()))
    when(home != c, block_out.wait_send)

    def sent(j):
        rs(j).wait_send()
        when(relays, give(j).wait_send)

        @pl.when(jnp.logical_not(relays))
        def _():
            for core in range(2):
                when(z < nz - 1, up(core, j).wait_send)
                across(core, j).wait_send()

    drained(jnp.logical_not(edge), 0, (nz - 1) * parts)
    each(half, sent)
    when(relays, lend.wait_send)

    @pl.when(jnp.logical_not(relays))
    def _():
        for rows in range(2):
            for n in range(len(sections)):
                att_copy(n, rows).wait_send()


def fused(nz, queries, keys, values, out_weight):
    frames_here, rows_here, columns, features = queries.shape
    tokens = frames_here * rows_here * columns
    heads, half, wide = features // HD, features // HD // 2, out_weight.shape[1]
    slots = nz // 2
    chunks = 2 * PIECES
    parts = PIECES
    width = wide // chunks
    vmem, hbm = pl.BlockSpec(memory_space=pltpu.VMEM), pl.BlockSpec(memory_space=pl.ANY)
    bf16, f32 = jnp.bfloat16, jnp.float32
    dma = pltpu.SemaphoreType.DMA
    def keep(array):
        return pltpu.with_memory_space_constraint(array, pltpu.HBM)

    out = pl.pallas_call(
        functools.partial(kernel, nz),
        out_shape=jax.ShapeDtypeStruct((tokens, slots * wide), bf16),
        in_specs=[hbm] * 4,
        out_specs=vmem,
        scratch_shapes=[
            pltpu.VMEM((2, tokens, features), bf16),
            pltpu.VMEM((tokens, features), bf16),
            pltpu.VMEM((tokens, features), bf16),
            pltpu.VMEM((features, tokens), bf16),
            pltpu.VMEM((nz, 2, chunks, width, features), bf16),
            pltpu.VMEM((2, tokens, features), bf16),
            pltpu.VMEM((heads, HD, LANES), f32),
            pltpu.VMEM((2, half, HD, LANES), f32),
            pltpu.VMEM((heads, HD, LANES), bf16),
            pltpu.VMEM((2, half, HD, LANES), bf16),
            pltpu.VMEM((half, HD, LANES), bf16),
            pltpu.VMEM((2, half, HD, LANES), bf16),
            pltpu.VMEM((2, half, HD, LANES), bf16),
            pltpu.VMEM((2, heads, HD, LANES), bf16),
            pltpu.VMEM((features, features), bf16),
            pltpu.VMEM((features, features), bf16),
            dma((5,)),
            dma((nz, 4, parts)),
            dma((3, parts)),
            dma((nz, 6, parts)),
            dma((3,)),
            dma((half,)),
            dma((2, half)),
            dma((half,)),
            dma((half,)),
            dma((2, half)),
            dma((2, half)),
            dma((2, half)),
            dma((2, half)),
            dma((2, 2)),
            dma((2, 2)),
        ],
        compiler_params=pltpu.CompilerParams(
            collective_id=0, has_side_effects=True, vmem_limit_bytes=30 * 2**20),
        name="attend_project",
    )(
        keep(queries.reshape(tokens, features)),
        keep(keys.reshape(tokens, features)),
        keep(values.reshape(tokens, features)),
        keep(out_weight.T.reshape(chunks, width, features)),
    )
    return out.reshape(frames_here, rows_here, columns, slots * wide)


def solution(mesh):
    size = dict(mesh.shape)
    pairs = size["rows"] == 2 and size["groups"] == 2 and size["heads"] == 2
    body = general
    if pairs and size["frames"] == 4:
        body = functools.partial(fused, size["frames"])
    return jax.shard_map(
        body,
        mesh=mesh,
        in_specs=(
            P(("groups", "frames"), "rows", None, "heads"),
            P(("groups", "frames"), "rows", None, "heads"),
            P(("groups", "frames"), "rows", None, "heads"),
            P("heads", "frames"),
        ),
        out_specs=P(("groups", "frames"), "rows", None, "heads"),
        check_vma=False,
    )
```

```python
import functools

import jax
import jax.numpy as jnp
from jax import lax
from jax.experimental import pallas as pl
from jax.experimental.pallas import tpu as pltpu
from jax.sharding import PartitionSpec as P

HD = 112
EPS = 1e-06
LANES = 128
MESH = pl.DeviceIdType.MESH


def prefix_before(local):
    position = lax.axis_index("frames") * local[0].shape[0]
    pieces = (
        lax.all_gather(local[0], "frames", axis=0, tiled=True),
        lax.all_gather(local[1], "frames", axis=0, tiled=True),
    )
    count = pieces[0].shape[0]
    keep = jnp.arange(count, dtype=jnp.int32) < position
    states = jnp.sum(jnp.where(keep[:, None, None, None], pieces[0], 0.0), axis=0, keepdims=True)
    totals = jnp.sum(jnp.where(keep[:, None, None], pieces[1], 0.0), axis=0, keepdims=True)
    return (states, totals)


def general(queries, keys, values, out_weight):
    frames_here, rows_here, columns, features = queries.shape
    heads_here = features // HD
    shape4 = (frames_here, rows_here * columns, heads_here, HD)
    query_pos = jnp.maximum(queries, 0).reshape(shape4).astype(jnp.float32)
    key_pos = jnp.maximum(keys, 0).reshape(shape4)
    value_rows = values.reshape(shape4)
    frame_state = jnp.einsum(
        "fthd,fthe->fhde", key_pos, value_rows, preferred_element_type=jnp.float32
    )
    frame_norm = jnp.sum(key_pos.astype(jnp.float32), axis=1)
    own = lax.psum((frame_state, frame_norm), "rows")
    earlier = prefix_before(own)
    state = own[0] + earlier[0]
    norm = own[1] + earlier[1]
    numer = jnp.einsum("fthd,fhde->fthe", query_pos, state, precision=lax.Precision.HIGHEST)
    denom = jnp.einsum("fthd,fhd->fth", query_pos, norm, precision=lax.Precision.HIGHEST)
    attended = (numer / (denom[..., None] + EPS)).astype(jnp.bfloat16)
    attended = attended.reshape(frames_here * rows_here * columns, features)
    terms = jnp.dot(
        attended,
        lax.all_gather(out_weight, "frames", axis=1, tiled=True),
        preferred_element_type=jnp.float32,
    )
    mixed = lax.psum_scatter(terms, "heads", scatter_dimension=1, tiled=True).astype(jnp.bfloat16)
    return mixed.reshape(frames_here, rows_here, columns, mixed.shape[1])


A, D, X, Y = 0, 1, 2, 3
PIECES = 5
OVER_Z, NEAR_X, FAR_X = 3, 1, 2
LAG, LAG_MID, LAG_Z = 3, 10, 5


def kernel(
    nz, q_hbm, k_hbm, v_hbm, w_ref, out_ref,
    q_ref, k_ref, v_ref, kt, wbuf, att, st, acc, rs_send, rs_recv, hand, z_recv, fin_send, fin, fmat, nmat,
    in_sem, w_recv, own_send, rel_send, block_sem, rs_out, rs_in, hand_out, hand_in, z_out, z_in,
    ag_out, fin_in, at_out, at_in,
):
    y, z = lax.axis_index("groups"), lax.axis_index("frames")
    x, c = lax.axis_index("rows"), lax.axis_index("heads")
    chunks = w_ref.shape[0]
    tokens, features = k_ref.shape
    wide = w_ref.shape[0] * w_ref.shape[1]
    heads = features // HD
    half = heads // 2
    parts = chunks // 2
    slots = nz // 2
    home = z // slots
    relays = c == x
    f32, bf16 = jnp.float32, jnp.bfloat16

    def dev(x_=None, y_=None, z_=None, c_=None):
        return (
            y if y_ is None else y_,
            z if z_ is None else z_,
            x if x_ is None else x_,
            c if c_ is None else c_,
        )

    def when(wanted, act):
        @pl.when(wanted)
        def _():
            act()

    partner = dev(c_=1 - c)
    barrier = pltpu.get_barrier_semaphore()

    def greet(device):
        pl.semaphore_signal(barrier, inc=1, device_id=device, device_id_type=MESH)

    greet(partner)
    for core in range(2):
        greet(dev(x_=1 - x, c_=core))
        greet(dev(y_=1 - y, c_=core))
    for side in (-1, 1):
        @pl.when((z + side >= 0) & (z + side < nz))
        def _():
            for core in range(2):
                greet(dev(z_=z + side, c_=core))

    loads = [
        pltpu.make_async_copy(src, dst, in_sem.at[n])
        for n, (src, dst) in enumerate(((k_hbm, k_ref), (v_hbm, v_ref), (q_hbm, q_ref.at[c])))
    ]
    loads[0].start()
    loads[1].start()
    when(c != x, loads[2].start)

    pl.semaphore_wait(barrier, jnp.where((z > 0) & (z < nz - 1), 9, 7))

    def remote(src, dst, send, recv, device):
        return pltpu.make_async_remote_copy(
            src_ref=src, dst_ref=dst, send_sem=send, recv_sem=recv,
            device_id=device, device_id_type=MESH,
        )

    def each(count, act, begin=0):
        def body(j, carry):
            act(j)
            return carry
        lax.fori_loop(begin, count, body, 0)

    mine = lax.rem(x + y + c, 2)
    kind = jnp.where(relays, A, D)

    def own_copy(side, j):
        chunk = mine * parts + j
        return remote(
            w_ref.at[chunk],
            wbuf.at[z, c, chunk],
            own_send.at[side, j],
            w_recv.at[z, kind, j],
            dev(z_=z + 1 - 2 * side, c_=x),
        )

    def own_each(act):
        for side in range(2):
            @pl.when((z < nz - 1) if side == 0 else (z > 0))
            def _():
                each(parts, lambda j: act(own_copy(side, j)))

    when(relays, lambda: own_each(lambda copy: copy.start()))

    def near_copy(j):
        chunk = mine * parts + j
        return remote(
            w_ref.at[chunk],
            wbuf.at[z, c, chunk],
            own_send.at[2, j],
            w_recv.at[z, D, j],
            dev(z_=jnp.where(z == 1, 0, nz - 1), c_=home),
        )

    def near_each(act):
        @pl.when(jnp.logical_not(relays) & ((z == 1) | (z == nz - 2)))
        def _():
            each(OVER_Z, lambda j: act(near_copy(j)))

    block_local = pltpu.make_async_copy(w_ref, wbuf.at[z, c], block_sem.at[0])
    block_out = remote(w_ref, wbuf.at[z, c], block_sem.at[1], block_sem.at[2], partner)
    lend = remote(q_hbm, q_ref.at[c], in_sem.at[3], in_sem.at[4], partner)
    when(relays, lend.start)
    when(home == c, block_local.start)
    when(home != c, block_out.start)

    base = {A: (x, y * parts), D: (1 - x, (1 - y) * parts),
            X: (1 - x, y * parts), Y: (x, (1 - y) * parts)}

    def relay(s, what, j, lane, to_kind, device):
        rows, first = base[what]
        ref = wbuf.at[s, rows, first + j]
        return remote(ref, ref, rel_send.at[s, lane, j], w_recv.at[s, to_kind, j], device)

    def arrived(s, what, j):
        relay(s, what, j, 0, what, partner).wait_recv()

    def place(s):
        to = jnp.where(s < z, z + 1, z - 1)
        then = jnp.where(s < z, z + 2, z - 2)
        ends = (s == 0) | (s == nz - 1)
        more = (to >= 0) & (to < nz)
        last = (then < 0) | (then >= nz)
        return ends, more, last, jnp.clip(to, 0, nz - 1), s // slots

    edge = (z == 0) | (z == nz - 1)

    def split(s, j):
        close = jnp.abs(s - z) == 1
        direct = jnp.where(edge & close, OVER_Z, 0)
        turned = direct + jnp.where(close, NEAR_X, FAR_X)
        plane = (s > 0) & (s < nz - 1) & (j >= direct)
        return plane & (j < turned), plane & (j >= turned)

    def sends_a(s, j):
        ends, more, last, to, at = place(s)
        over_x, over_y = split(s, j)
        x_core = jnp.where(over_y, 1 - x, at)
        y_core = jnp.where(over_x, x, at)
        return (
            (more, relay(s, A, j, 2, A, dev(z_=to, c_=x))),
            (None, relay(s, A, j, 0, X, dev(x_=1 - x, c_=x_core))),
            (None, relay(s, A, j, 1, Y, dev(y_=1 - y, c_=y_core))),
            (at != x, relay(s, A, j, 4, A, partner)),
        )

    def sends_d(s, j):
        ends, more, last, to, at = place(s)
        far = ends & more
        over_x, over_y = split(s, j)
        z_core = jnp.where(last, at, x)
        return (
            (over_x, Y, relay(s, Y, j, 3, D, dev(x_=1 - x, c_=at)), relay(s, Y, j, 5, Y, partner)),
            (over_y, X, relay(s, X, j, 3, D, dev(y_=1 - y, c_=at)), relay(s, X, j, 5, X, partner)),
            (far, D, relay(s, D, j, 3, D, dev(z_=to, c_=z_core)), relay(s, D, j, 5, D, partner)),
        ), at != x

    def around(d, act):
        for side in (-1, 1):
            s = z + side * d
            when((s >= 0) & (s < nz), lambda: act(jnp.clip(s, 0, nz - 1)))

    def on_a(s, j):
        arrived(s, A, j)
        for needed, copy in sends_a(s, j):
            if needed is None:
                copy.start()
            else:
                when(needed, copy.start)

    def on_d(s, j, along):
        options, share = sends_d(s, j)
        for wanted, what, copy, inner in options[2:] if along else options[:2]:
            @pl.when(wanted)
            def _():
                arrived(s, what, j)
                copy.start()
                when(share, inner.start)

    def drain(s, j):
        for needed, copy in sends_a(s, j):
            if needed is None:
                copy.wait_send()
            else:
                when(needed, copy.wait_send)
        options, share = sends_d(s, j)
        for wanted, what, copy, inner in options:
            @pl.when(wanted)
            def _():
                copy.wait_send()
                when(share, inner.wait_send)

    def rs(j):
        return remote(rs_send.at[(1 - x) * half + j], rs_recv.at[c, j], rs_out.at[j], rs_in.at[c, j],
                      dev(x_=1 - x, c_=x))

    def give(j):
        return remote(rs_send.at[x * half + j], hand.at[j], hand_out.at[j], hand_in.at[j], partner)

    loads[0].wait()
    kt[...] = jnp.maximum(k_ref[...], 0).T
    loads[1].wait()
    ones = jnp.ones((tokens, LANES), bf16)
    for j in range(half):
        for h in (j, half + j):
            first = h * HD
            begin = first // LANES * LANES
            end = min(-(-(first + HD) // LANES) * LANES, features)
            kp = kt[first:first + HD, :]
            both = jnp.dot(kp, v_ref[:, begin:end], preferred_element_type=f32)
            total = jnp.dot(kp, ones, preferred_element_type=f32)
            st[h, :, :HD] = both[:, first - begin:first - begin + HD]
            st[h, :, HD:] = total[:, HD:]
            rs_send[h] = st[h].astype(bf16)
        rs(j).start()
        when(relays, give(j).start)

    fmat[...] = jnp.zeros_like(fmat)
    nmat[...] = jnp.zeros_like(nmat)

    def up(core, j):
        return remote(fin_send.at[core, j], z_recv.at[core, j], z_out.at[core, j], z_in.at[core, j],
                      dev(z_=jnp.minimum(z + 1, nz - 1)))

    def across(core, j):
        return remote(fin_send.at[core, j], fin.at[core, x * half + j], ag_out.at[core, j], fin_in.at[core, j],
                      dev(x_=1 - x, c_=x))

    def gather_step(j):
        for core in range(2):
            pltpu_wait = remote(rs_recv.at[core, j], rs_recv.at[core, j], rs_out.at[j], rs_in.at[core, j], partner)
            pltpu_wait.wait_recv()

            @pl.when(c == core)
            def _():
                acc[core, j] = st[x * half + j] + rs_recv[core, j].astype(f32)

            @pl.when(c != core)
            def _():
                give(j).wait_recv()
                acc[core, j] = hand[j].astype(f32) + rs_recv[core, j].astype(f32)

    def chain_step(j):
        for core in range(2):
            @pl.when(z > 0)
            def _():
                up(core, j).wait_recv()
                acc[core, j] = acc[core, j] + z_recv[core, j].astype(f32)
            fin_send[core, j] = acc[core, j].astype(bf16)
            when(z < nz - 1, up(core, j).start)
            across(core, j).start()
            fin[core, x * half + j] = fin_send[core, j]

    @pl.when(jnp.logical_not(relays))
    def _():
        each(half, gather_step)
        when(z == nz - 1, lambda: own_each(lambda copy: copy.start()))
        each(half, chain_step)
        when(z == 0, lambda: own_each(lambda copy: copy.start()))

    cuts = []
    for begin in range(0, features, 2 * LANES):
        end = min(begin + 2 * LANES, features)
        low = begin // HD * HD // LANES * LANES
        high = min(-(-(-(-end // HD) * HD) // LANES) * LANES, features)
        cuts.append((begin, end, low, high))

    sections = ((0, 4 * LANES), (4 * LANES, features))

    def att_copy(n, rows):
        begin, end = sections[n]
        ref = att.at[rows, :, begin:end]
        return remote(ref, ref, at_out.at[rows, n], at_in.at[rows, n], partner)

    def attend(turn):
        rows = lax.rem(c + turn, 2)

        def finished(j):
            ref = fin.at[rows, (1 - x) * half + j]
            remote(ref, ref, ag_out.at[rows, j], fin_in.at[rows, j], partner).wait_recv()

        each(half, finished)
        for h in range(heads):
            own = slice(h * HD, (h + 1) * HD)
            block = fin[rows, h]
            fmat[own, own] = block[:, :HD]
            nmat[own, own] = jnp.broadcast_to(block[:, HD:HD + 1], (HD, HD))
        sent = 0
        for begin, end, low, high in cuts:
            qp = jnp.maximum(q_ref[rows, :, low:high], 0)
            numer = jnp.dot(qp, fmat[low:high, begin:end], preferred_element_type=f32)
            denom = jnp.dot(qp, nmat[low:high, begin:end], preferred_element_type=f32)
            att[rows, :, begin:end] = (numer / (denom + EPS)).astype(bf16)
            if end == sections[sent][1]:
                att_copy(sent, rows).start()
                sent += 1

    @pl.when(jnp.logical_not(relays))
    def _():
        loads[2].wait()
        remote(q_hbm, q_ref.at[1 - c], in_sem.at[3], in_sem.at[4], partner).wait_recv()
        each(2, attend)

    def step(t):
        d, j = t // parts + 1, lax.rem(t, parts)

        @pl.when(relays)
        def _():
            when(d < nz, lambda: around(d, lambda s: on_a(s, j)))
            for lag, along in ((jnp.where(edge, LAG, LAG_MID), False), (LAG_Z, True)):
                late = t - lag

                @pl.when((late >= 0) & (late < (nz - 1) * parts))
                def _():
                    around(late // parts + 1, lambda s: on_d(s, lax.rem(late, parts), along))

    each((nz - 1) * parts + max(LAG, LAG_Z), step)
    near_each(lambda copy: copy.start())

    @pl.when(relays)
    def _():
        for rows in range(2):
            for n in range(len(sections)):
                att_copy(n, rows).wait_recv()

    def slot(i):
        s = jnp.where(z <= slots * c, i, slots - 1 - i)
        return s, slots * c + s

    def landed(s, j, kinds):
        ends, more, last, to, at = place(s)
        over_x, over_y = split(s, j)
        held = {A: relays, X: relays & over_y, Y: relays & over_x, D: relays & ends & more}
        for what in kinds:
            when(jnp.logical_not(held[what]), lambda: arrived(s, what, j))

    def product(rows, weights):
        return lax.dot_general(att[rows], weights, (((1,), (1,)), ((), ())), preferred_element_type=f32)

    def drained(wanted, begin, end):
        @pl.when(relays & wanted)
        def _():
            each(end, lambda t: around(t // parts + 1, lambda s: drain(s, lax.rem(t, parts))), begin)

    width = wide // 2

    def quarter(source, rows, first):
        return wbuf[source, rows, pl.ds(first, parts)].reshape(width, features)

    def await_all(source, kinds):
        each(parts, lambda j: landed(source, j, kinds))

    def put(s, side, value):
        value = value.astype(out_ref.dtype)
        for at in range(slots):
            for part in range(2):
                first = (at * 2 + part) * width

                @pl.when((s == at) & (side == part))
                def _():
                    out_ref[:, first:first + width] = value

    def near(i):
        s, source = slot(i)
        await_all(source, (A, X))
        put(s, y, product(x, quarter(source, x, y * parts)) + product(1 - x, quarter(source, 1 - x, y * parts)))

    def distant(i):
        s, source = slot(i)
        await_all(source, (D,))
        rest = product(1 - x, quarter(source, 1 - x, (1 - y) * parts))
        await_all(source, (Y,))
        put(s, 1 - y, rest + product(x, quarter(source, x, (1 - y) * parts)))

    @pl.when(home == c)
    def _():
        s, source = slot(0)
        block_local.wait()
        other = wbuf.at[z, 1 - c]
        remote(w_ref, other, block_sem.at[1], block_sem.at[2], partner).wait_recv()
        out = product(0, wbuf[source, 0].reshape(wide, features))
        out = (out + product(1, wbuf[source, 1].reshape(wide, features))).astype(out_ref.dtype)
        for at in range(slots):
            @pl.when(s == at)
            def _():
                out_ref[:, at * wide:(at + 1) * wide] = out

    @pl.when(home != c)
    def _():
        near(0)

    drained(edge, 0, (nz - 2) * parts)
    when(home != c, lambda: distant(0))
    near(slots - 1)
    drained(edge, (nz - 2) * parts, (nz - 1) * parts)
    distant(slots - 1)

    near_each(lambda copy: copy.wait_send())
    when(relays | (z == 0) | (z == nz - 1), lambda: own_each(lambda copy: copy.wait_send()))
    when(home != c, block_out.wait_send)

    def sent(j):
        rs(j).wait_send()
        when(relays, give(j).wait_send)

        @pl.when(jnp.logical_not(relays))
        def _():
            for core in range(2):
                when(z < nz - 1, up(core, j).wait_send)
                across(core, j).wait_send()

    drained(jnp.logical_not(edge), 0, (nz - 1) * parts)
    each(half, sent)
    when(relays, lend.wait_send)

    @pl.when(jnp.logical_not(relays))
    def _():
        for rows in range(2):
            for n in range(len(sections)):
                att_copy(n, rows).wait_send()


def fused(nz, queries, keys, values, out_weight):
    frames_here, rows_here, columns, features = queries.shape
    tokens = frames_here * rows_here * columns
    heads, half, wide = features // HD, features // HD // 2, out_weight.shape[1]
    slots = nz // 2
    chunks = 2 * PIECES
    parts = PIECES
    width = wide // chunks
    vmem, hbm = pl.BlockSpec(memory_space=pltpu.VMEM), pl.BlockSpec(memory_space=pl.ANY)
    bf16, f32 = jnp.bfloat16, jnp.float32
    dma = pltpu.SemaphoreType.DMA
    def keep(array):
        return pltpu.with_memory_space_constraint(array, pltpu.HBM)

    out = pl.pallas_call(
        functools.partial(kernel, nz),
        out_shape=jax.ShapeDtypeStruct((tokens, slots * wide), bf16),
        in_specs=[hbm] * 4,
        out_specs=vmem,
        scratch_shapes=[
            pltpu.VMEM((2, tokens, features), bf16),
            pltpu.VMEM((tokens, features), bf16),
            pltpu.VMEM((tokens, features), bf16),
            pltpu.VMEM((features, tokens), bf16),
            pltpu.VMEM((nz, 2, chunks, width, features), bf16),
            pltpu.VMEM((2, tokens, features), bf16),
            pltpu.VMEM((heads, HD, LANES), f32),
            pltpu.VMEM((2, half, HD, LANES), f32),
            pltpu.VMEM((heads, HD, LANES), bf16),
            pltpu.VMEM((2, half, HD, LANES), bf16),
            pltpu.VMEM((half, HD, LANES), bf16),
            pltpu.VMEM((2, half, HD, LANES), bf16),
            pltpu.VMEM((2, half, HD, LANES), bf16),
            pltpu.VMEM((2, heads, HD, LANES), bf16),
            pltpu.VMEM((features, features), bf16),
            pltpu.VMEM((features, features), bf16),
            dma((5,)),
            dma((nz, 4, parts)),
            dma((3, parts)),
            dma((nz, 6, parts)),
            dma((3,)),
            dma((half,)),
            dma((2, half)),
            dma((half,)),
            dma((half,)),
            dma((2, half)),
            dma((2, half)),
            dma((2, half)),
            dma((2, half)),
            dma((2, 2)),
            dma((2, 2)),
        ],
        compiler_params=pltpu.CompilerParams(
            collective_id=0, has_side_effects=True, vmem_limit_bytes=30 * 2**20),
        name="attend_project",
    )(
        keep(queries.reshape(tokens, features)),
        keep(keys.reshape(tokens, features)),
        keep(values.reshape(tokens, features)),
        keep(out_weight.T.reshape(chunks, width, features)),
    )
    return out.reshape(frames_here, rows_here, columns, slots * wide)


def solution(mesh):
    size = dict(mesh.shape)
    pairs = size["rows"] == 2 and size["groups"] == 2 and size["heads"] == 2
    body = general
    if pairs and size["frames"] == 4:
        body = functools.partial(fused, size["frames"])
    return jax.shard_map(
        body,
        mesh=mesh,
        in_specs=(
            P(("groups", "frames"), "rows", None, "heads"),
            P(("groups", "frames"), "rows", None, "heads"),
            P(("groups", "frames"), "rows", None, "heads"),
            P("heads", "frames"),
        ),
        out_specs=P(("groups", "frames"), "rows", None, "heads"),
        check_vma=False,
    )
```

```python
import functools

import jax
import jax.numpy as jnp
from jax import lax
from jax.experimental import pallas as pl
from jax.experimental.pallas import tpu as pltpu
from jax.sharding import PartitionSpec as P

HD = 112
EPS = 1e-06
LANES = 128
MESH = pl.DeviceIdType.MESH


def prefix_before(local):
    position = lax.axis_index("frames") * local[0].shape[0]
    pieces = (
        lax.all_gather(local[0], "frames", axis=0, tiled=True),
        lax.all_gather(local[1], "frames", axis=0, tiled=True),
    )
    count = pieces[0].shape[0]
    keep = jnp.arange(count, dtype=jnp.int32) < position
    states = jnp.sum(jnp.where(keep[:, None, None, None], pieces[0], 0.0), axis=0, keepdims=True)
    totals = jnp.sum(jnp.where(keep[:, None, None], pieces[1], 0.0), axis=0, keepdims=True)
    return (states, totals)


def general(queries, keys, values, out_weight):
    frames_here, rows_here, columns, features = queries.shape
    heads_here = features // HD
    shape4 = (frames_here, rows_here * columns, heads_here, HD)
    query_pos = jnp.maximum(queries, 0).reshape(shape4).astype(jnp.float32)
    key_pos = jnp.maximum(keys, 0).reshape(shape4)
    value_rows = values.reshape(shape4)
    frame_state = jnp.einsum(
        "fthd,fthe->fhde", key_pos, value_rows, preferred_element_type=jnp.float32
    )
    frame_norm = jnp.sum(key_pos.astype(jnp.float32), axis=1)
    own = lax.psum((frame_state, frame_norm), "rows")
    earlier = prefix_before(own)
    state = own[0] + earlier[0]
    norm = own[1] + earlier[1]
    numer = jnp.einsum("fthd,fhde->fthe", query_pos, state, precision=lax.Precision.HIGHEST)
    denom = jnp.einsum("fthd,fhd->fth", query_pos, norm, precision=lax.Precision.HIGHEST)
    attended = (numer / (denom[..., None] + EPS)).astype(jnp.bfloat16)
    attended = attended.reshape(frames_here * rows_here * columns, features)
    terms = jnp.dot(
        attended,
        lax.all_gather(out_weight, "frames", axis=1, tiled=True),
        preferred_element_type=jnp.float32,
    )
    mixed = lax.psum_scatter(terms, "heads", scatter_dimension=1, tiled=True).astype(jnp.bfloat16)
    return mixed.reshape(frames_here, rows_here, columns, mixed.shape[1])


A, D, X, Y = 0, 1, 2, 3
PIECES = 5
OVER_Z, NEAR_X, FAR_X = 3, 1, 2
LAG, LAG_MID, LAG_Z = 3, 10, 5


def kernel(
    nz, q_hbm, k_hbm, v_hbm, w_ref, out_ref,
    q_ref, k_ref, v_ref, kt, wbuf, att, st, acc, rs_send, rs_recv, hand, z_recv, fin_send, fin, fmat, nmat,
    in_sem, w_recv, own_send, rel_send, block_sem, rs_out, rs_in, hand_out, hand_in, z_out, z_in,
    ag_out, fin_in, at_out, at_in,
):
    y, z = lax.axis_index("groups"), lax.axis_index("frames")
    x, c = lax.axis_index("rows"), lax.axis_index("heads")
    chunks = w_ref.shape[0]
    tokens, features = k_ref.shape
    wide = w_ref.shape[0] * w_ref.shape[1]
    heads = features // HD
    half = heads // 2
    parts = chunks // 2
    slots = nz // 2
    home = z // slots
    relays = c == x
    f32, bf16 = jnp.float32, jnp.bfloat16

    def dev(x_=None, y_=None, z_=None, c_=None):
        return (
            y if y_ is None else y_,
            z if z_ is None else z_,
            x if x_ is None else x_,
            c if c_ is None else c_,
        )

    def when(wanted, act):
        @pl.when(wanted)
        def _():
            act()

    partner = dev(c_=1 - c)
    barrier = pltpu.get_barrier_semaphore()

    def greet(device):
        pl.semaphore_signal(barrier, inc=1, device_id=device, device_id_type=MESH)

    greet(partner)
    for core in range(2):
        greet(dev(x_=1 - x, c_=core))
        greet(dev(y_=1 - y, c_=core))
    for side in (-1, 1):
        @pl.when((z + side >= 0) & (z + side < nz))
        def _():
            for core in range(2):
                greet(dev(z_=z + side, c_=core))

    loads = [
        pltpu.make_async_copy(src, dst, in_sem.at[n])
        for n, (src, dst) in enumerate(((k_hbm, k_ref), (v_hbm, v_ref), (q_hbm, q_ref.at[c])))
    ]
    loads[0].start()
    loads[1].start()
    when(c != x, loads[2].start)

    pl.semaphore_wait(barrier, jnp.where((z > 0) & (z < nz - 1), 9, 7))

    def remote(src, dst, send, recv, device):
        return pltpu.make_async_remote_copy(
            src_ref=src, dst_ref=dst, send_sem=send, recv_sem=recv,
            device_id=device, device_id_type=MESH,
        )

    def each(count, act, begin=0):
        def body(j, carry):
            act(j)
            return carry
        lax.fori_loop(begin, count, body, 0)

    mine = lax.rem(x + y + c, 2)
    kind = jnp.where(relays, A, D)

    def own_copy(side, j):
        chunk = mine * parts + j
        return remote(
            w_ref.at[chunk],
            wbuf.at[z, c, chunk],
            own_send.at[side, j],
            w_recv.at[z, kind, j],
            dev(z_=z + 1 - 2 * side, c_=x),
        )

    def own_each(act):
        for side in range(2):
            @pl.when((z < nz - 1) if side == 0 else (z > 0))
            def _():
                each(parts, lambda j: act(own_copy(side, j)))

    when(relays, lambda: own_each(lambda copy: copy.start()))

    def near_copy(j):
        chunk = mine * parts + j
        return remote(
            w_ref.at[chunk],
            wbuf.at[z, c, chunk],
            own_send.at[2, j],
            w_recv.at[z, D, j],
            dev(z_=jnp.where(z == 1, 0, nz - 1), c_=home),
        )

    def near_each(act):
        @pl.when(jnp.logical_not(relays) & ((z == 1) | (z == nz - 2)))
        def _():
            each(OVER_Z, lambda j: act(near_copy(j)))

    block_local = pltpu.make_async_copy(w_ref, wbuf.at[z, c], block_sem.at[0])
    block_out = remote(w_ref, wbuf.at[z, c], block_sem.at[1], block_sem.at[2], partner)
    lend = remote(q_hbm, q_ref.at[c], in_sem.at[3], in_sem.at[4], partner)
    when(relays, lend.start)
    when(home == c, block_local.start)
    when(home != c, block_out.start)

    base = {A: (x, y * parts), D: (1 - x, (1 - y) * parts),
            X: (1 - x, y * parts), Y: (x, (1 - y) * parts)}

    def relay(s, what, j, lane, to_kind, device):
        rows, first = base[what]
        ref = wbuf.at[s, rows, first + j]
        return remote(ref, ref, rel_send.at[s, lane, j], w_recv.at[s, to_kind, j], device)

    def arrived(s, what, j):
        relay(s, what, j, 0, what, partner).wait_recv()

    def place(s):
        to = jnp.where(s < z, z + 1, z - 1)
        then = jnp.where(s < z, z + 2, z - 2)
        ends = (s == 0) | (s == nz - 1)
        more = (to >= 0) & (to < nz)
        last = (then < 0) | (then >= nz)
        return ends, more, last, jnp.clip(to, 0, nz - 1), s // slots

    edge = (z == 0) | (z == nz - 1)

    def split(s, j):
        close = jnp.abs(s - z) == 1
        direct = jnp.where(edge & close, OVER_Z, 0)
        turned = direct + jnp.where(close, NEAR_X, FAR_X)
        plane = (s > 0) & (s < nz - 1) & (j >= direct)
        return plane & (j < turned), plane & (j >= turned)

    def sends_a(s, j):
        ends, more, last, to, at = place(s)
        over_x, over_y = split(s, j)
        x_core = jnp.where(over_y, 1 - x, at)
        y_core = jnp.where(over_x, x, at)
        return (
            (more, relay(s, A, j, 2, A, dev(z_=to, c_=x))),
            (None, relay(s, A, j, 0, X, dev(x_=1 - x, c_=x_core))),
            (None, relay(s, A, j, 1, Y, dev(y_=1 - y, c_=y_core))),
            (at != x, relay(s, A, j, 4, A, partner)),
        )

    def sends_d(s, j):
        ends, more, last, to, at = place(s)
        far = ends & more
        over_x, over_y = split(s, j)
        z_core = jnp.where(last, at, x)
        return (
            (over_x, Y, relay(s, Y, j, 3, D, dev(x_=1 - x, c_=at)), relay(s, Y, j, 5, Y, partner)),
            (over_y, X, relay(s, X, j, 3, D, dev(y_=1 - y, c_=at)), relay(s, X, j, 5, X, partner)),
            (far, D, relay(s, D, j, 3, D, dev(z_=to, c_=z_core)), relay(s, D, j, 5, D, partner)),
        ), at != x

    def around(d, act):
        for side in (-1, 1):
            s = z + side * d
            when((s >= 0) & (s < nz), lambda: act(jnp.clip(s, 0, nz - 1)))

    def on_a(s, j):
        arrived(s, A, j)
        for needed, copy in sends_a(s, j):
            if needed is None:
                copy.start()
            else:
                when(needed, copy.start)

    def on_d(s, j, along):
        options, share = sends_d(s, j)
        for wanted, what, copy, inner in options[2:] if along else options[:2]:
            @pl.when(wanted)
            def _():
                arrived(s, what, j)
                copy.start()
                when(share, inner.start)

    def drain(s, j):
        for needed, copy in sends_a(s, j):
            if needed is None:
                copy.wait_send()
            else:
                when(needed, copy.wait_send)
        options, share = sends_d(s, j)
        for wanted, what, copy, inner in options:
            @pl.when(wanted)
            def _():
                copy.wait_send()
                when(share, inner.wait_send)

    def rs(j):
        return remote(rs_send.at[(1 - x) * half + j], rs_recv.at[c, j], rs_out.at[j], rs_in.at[c, j],
                      dev(x_=1 - x, c_=x))

    def give(j):
        return remote(rs_send.at[x * half + j], hand.at[j], hand_out.at[j], hand_in.at[j], partner)

    loads[0].wait()
    kt[...] = jnp.maximum(k_ref[...], 0).T
    loads[1].wait()
    ones = jnp.ones((tokens, LANES), bf16)
    for j in range(half):
        for h in (j, half + j):
            first = h * HD
            begin = first // LANES * LANES
            end = min(-(-(first + HD) // LANES) * LANES, features)
            kp = kt[first:first + HD, :]
            both = jnp.dot(kp, v_ref[:, begin:end], preferred_element_type=f32)
            total = jnp.dot(kp, ones, preferred_element_type=f32)
            st[h, :, :HD] = both[:, first - begin:first - begin + HD]
            st[h, :, HD:] = total[:, HD:]
            rs_send[h] = st[h].astype(bf16)
        rs(j).start()
        when(relays, give(j).start)

    @pl.when(jnp.logical_not(relays))
    def _():
        fmat[...] = jnp.zeros_like(fmat)
        nmat[...] = jnp.zeros_like(nmat)

    def up(core, j):
        return remote(fin_send.at[core, j], z_recv.at[core, j], z_out.at[core, j], z_in.at[core, j],
                      dev(z_=jnp.minimum(z + 1, nz - 1)))

    def across(core, j):
        return remote(fin_send.at[core, j], fin.at[core, x * half + j], ag_out.at[core, j], fin_in.at[core, j],
                      dev(x_=1 - x, c_=x))

    def gather_step(j):
        for core in range(2):
            pltpu_wait = remote(rs_recv.at[core, j], rs_recv.at[core, j], rs_out.at[j], rs_in.at[core, j], partner)
            pltpu_wait.wait_recv()

            @pl.when(c == core)
            def _():
                acc[core, j] = st[x * half + j] + rs_recv[core, j].astype(f32)

            @pl.when(c != core)
            def _():
                give(j).wait_recv()
                acc[core, j] = hand[j].astype(f32) + rs_recv[core, j].astype(f32)

    def chain_step(j):
        for core in range(2):
            @pl.when(z > 0)
            def _():
                up(core, j).wait_recv()
                acc[core, j] = acc[core, j] + z_recv[core, j].astype(f32)
            fin_send[core, j] = acc[core, j].astype(bf16)
            when(z < nz - 1, up(core, j).start)
            across(core, j).start()
            fin[core, x * half + j] = fin_send[core, j]

    @pl.when(jnp.logical_not(relays))
    def _():
        each(half, gather_step)
        when(z == nz - 1, lambda: own_each(lambda copy: copy.start()))
        each(half, chain_step)
        when(z == 0, lambda: own_each(lambda copy: copy.start()))

    cuts = []
    for begin in range(0, features, 2 * LANES):
        end = min(begin + 2 * LANES, features)
        low = begin // HD * HD // LANES * LANES
        high = min(-(-(-(-end // HD) * HD) // LANES) * LANES, features)
        cuts.append((begin, end, low, high))

    sections = ((0, 4 * LANES), (4 * LANES, features))

    def att_copy(n, rows):
        begin, end = sections[n]
        ref = att.at[rows, :, begin:end]
        return remote(ref, ref, at_out.at[rows, n], at_in.at[rows, n], partner)

    def attend(turn):
        rows = lax.rem(c + turn, 2)

        def finished(j):
            ref = fin.at[rows, (1 - x) * half + j]
            remote(ref, ref, ag_out.at[rows, j], fin_in.at[rows, j], partner).wait_recv()

        each(half, finished)
        for h in range(heads):
            own = slice(h * HD, (h + 1) * HD)
            block = fin[rows, h]
            fmat[own, own] = block[:, :HD]
            nmat[own, own] = jnp.broadcast_to(block[:, HD:HD + 1], (HD, HD))
        sent = 0
        for begin, end, low, high in cuts:
            qp = jnp.maximum(q_ref[rows, :, low:high], 0)
            numer = jnp.dot(qp, fmat[low:high, begin:end], preferred_element_type=f32)
            denom = jnp.dot(qp, nmat[low:high, begin:end], preferred_element_type=f32)
            att[rows, :, begin:end] = (numer / (denom + EPS)).astype(bf16)
            if end == sections[sent][1]:
                att_copy(sent, rows).start()
                sent += 1

    @pl.when(jnp.logical_not(relays))
    def _():
        loads[2].wait()
        remote(q_hbm, q_ref.at[1 - c], in_sem.at[3], in_sem.at[4], partner).wait_recv()
        each(2, attend)

    def step(t):
        d, j = t // parts + 1, lax.rem(t, parts)

        @pl.when(relays)
        def _():
            when(d < nz, lambda: around(d, lambda s: on_a(s, j)))
            for lag, along in ((jnp.where(edge, LAG, LAG_MID), False), (LAG_Z, True)):
                late = t - lag

                @pl.when((late >= 0) & (late < (nz - 1) * parts))
                def _():
                    around(late // parts + 1, lambda s: on_d(s, lax.rem(late, parts), along))

    each((nz - 1) * parts + max(LAG, LAG_Z), step)
    near_each(lambda copy: copy.start())

    @pl.when(relays)
    def _():
        for rows in range(2):
            for n in range(len(sections)):
                att_copy(n, rows).wait_recv()

    def slot(i):
        s = jnp.where(z <= slots * c, i, slots - 1 - i)
        return s, slots * c + s

    def landed(s, j, kinds):
        ends, more, last, to, at = place(s)
        over_x, over_y = split(s, j)
        held = {A: relays, X: relays & over_y, Y: relays & over_x, D: relays & ends & more}
        for what in kinds:
            when(jnp.logical_not(held[what]), lambda: arrived(s, what, j))

    def product(rows, weights):
        return lax.dot_general(att[rows], weights, (((1,), (1,)), ((), ())), preferred_element_type=f32)

    def drained(wanted, begin, end):
        @pl.when(relays & wanted)
        def _():
            each(end, lambda t: around(t // parts + 1, lambda s: drain(s, lax.rem(t, parts))), begin)

    width = wide // 2

    def quarter(source, rows, first):
        return wbuf[source, rows, pl.ds(first, parts)].reshape(width, features)

    def await_all(source, kinds):
        each(parts, lambda j: landed(source, j, kinds))

    def put(s, side, value):
        value = value.astype(out_ref.dtype)
        for at in range(slots):
            for part in range(2):
                first = (at * 2 + part) * width

                @pl.when((s == at) & (side == part))
                def _():
                    out_ref[:, first:first + width] = value

    def near(i):
        s, source = slot(i)
        await_all(source, (A, X))
        put(s, y, product(x, quarter(source, x, y * parts)) + product(1 - x, quarter(source, 1 - x, y * parts)))

    def distant(i):
        s, source = slot(i)
        await_all(source, (D,))
        rest = product(1 - x, quarter(source, 1 - x, (1 - y) * parts))
        await_all(source, (Y,))
        put(s, 1 - y, rest + product(x, quarter(source, x, (1 - y) * parts)))

    @pl.when(home == c)
    def _():
        s, source = slot(0)
        block_local.wait()
        other = wbuf.at[z, 1 - c]
        remote(w_ref, other, block_sem.at[1], block_sem.at[2], partner).wait_recv()
        out = product(0, wbuf[source, 0].reshape(wide, features))
        out = (out + product(1, wbuf[source, 1].reshape(wide, features))).astype(out_ref.dtype)
        for at in range(slots):
            @pl.when(s == at)
            def _():
                out_ref[:, at * wide:(at + 1) * wide] = out

    @pl.when(home != c)
    def _():
        near(0)

    drained(edge, 0, (nz - 2) * parts)
    when(home != c, lambda: distant(0))
    near(slots - 1)
    drained(edge & (home != c), (nz - 2) * parts, (nz - 1) * parts)
    distant(slots - 1)
    drained(edge & (home == c), (nz - 2) * parts, (nz - 1) * parts)

    near_each(lambda copy: copy.wait_send())
    when(relays | (z == 0) | (z == nz - 1), lambda: own_each(lambda copy: copy.wait_send()))
    when(home != c, block_out.wait_send)

    def sent(j):
        rs(j).wait_send()
        when(relays, give(j).wait_send)

        @pl.when(jnp.logical_not(relays))
        def _():
            for core in range(2):
                when(z < nz - 1, up(core, j).wait_send)
                across(core, j).wait_send()

    drained(jnp.logical_not(edge), 0, (nz - 1) * parts)
    each(half, sent)
    when(relays, lend.wait_send)

    @pl.when(jnp.logical_not(relays))
    def _():
        for rows in range(2):
            for n in range(len(sections)):
                att_copy(n, rows).wait_send()


def fused(nz, queries, keys, values, out_weight):
    frames_here, rows_here, columns, features = queries.shape
    tokens = frames_here * rows_here * columns
    heads, half, wide = features // HD, features // HD // 2, out_weight.shape[1]
    slots = nz // 2
    chunks = 2 * PIECES
    parts = PIECES
    width = wide // chunks
    vmem, hbm = pl.BlockSpec(memory_space=pltpu.VMEM), pl.BlockSpec(memory_space=pl.ANY)
    bf16, f32 = jnp.bfloat16, jnp.float32
    dma = pltpu.SemaphoreType.DMA
    def keep(array):
        return pltpu.with_memory_space_constraint(array, pltpu.HBM)

    out = pl.pallas_call(
        functools.partial(kernel, nz),
        out_shape=jax.ShapeDtypeStruct((tokens, slots * wide), bf16),
        in_specs=[hbm] * 4,
        out_specs=vmem,
        scratch_shapes=[
            pltpu.VMEM((2, tokens, features), bf16),
            pltpu.VMEM((tokens, features), bf16),
            pltpu.VMEM((tokens, features), bf16),
            pltpu.VMEM((features, tokens), bf16),
            pltpu.VMEM((nz, 2, chunks, width, features), bf16),
            pltpu.VMEM((2, tokens, features), bf16),
            pltpu.VMEM((heads, HD, LANES), f32),
            pltpu.VMEM((2, half, HD, LANES), f32),
            pltpu.VMEM((heads, HD, LANES), bf16),
            pltpu.VMEM((2, half, HD, LANES), bf16),
            pltpu.VMEM((half, HD, LANES), bf16),
            pltpu.VMEM((2, half, HD, LANES), bf16),
            pltpu.VMEM((2, half, HD, LANES), bf16),
            pltpu.VMEM((2, heads, HD, LANES), bf16),
            pltpu.VMEM((features, features), bf16),
            pltpu.VMEM((features, features), bf16),
            dma((5,)),
            dma((nz, 4, parts)),
            dma((3, parts)),
            dma((nz, 6, parts)),
            dma((3,)),
            dma((half,)),
            dma((2, half)),
            dma((half,)),
            dma((half,)),
            dma((2, half)),
            dma((2, half)),
            dma((2, half)),
            dma((2, half)),
            dma((2, 2)),
            dma((2, 2)),
        ],
        compiler_params=pltpu.CompilerParams(
            collective_id=0, has_side_effects=True, vmem_limit_bytes=30 * 2**20),
        name="attend_project",
    )(
        keep(queries.reshape(tokens, features)),
        keep(keys.reshape(tokens, features)),
        keep(values.reshape(tokens, features)),
        keep(out_weight.T.reshape(chunks, width, features)),
    )
    return out.reshape(frames_here, rows_here, columns, slots * wide)


def solution(mesh):
    size = dict(mesh.shape)
    pairs = size["rows"] == 2 and size["groups"] == 2 and size["heads"] == 2
    body = general
    if pairs and size["frames"] == 4:
        body = functools.partial(fused, size["frames"])
    return jax.shard_map(
        body,
        mesh=mesh,
        in_specs=(
            P(("groups", "frames"), "rows", None, "heads"),
            P(("groups", "frames"), "rows", None, "heads"),
            P(("groups", "frames"), "rows", None, "heads"),
            P("heads", "frames"),
        ),
        out_specs=P(("groups", "frames"), "rows", None, "heads"),
        check_vma=False,
    )
```
